32 devices in a mesh: replica: 4 (over y, core), fsdp: 2 (over x), tensor: 4 (over z).
Axes of the slice: x: 2, y: 2, z: 4, core: 2. Of those that a mesh axis runs over, the one named last changes fastest.
Arguments:
- hidden: bfloat16 [1024, 8192], P(('replica', 'fsdp')), may hold values from -6 to 6
- key_weight: bfloat16 [4, 8192, 1024], P('replica', 'fsdp', 'tensor'), may hold values from -0.0625 to 0.0625
- key_grad: bfloat16 [1024, 1024], P(('replica', 'fsdp'), 'tensor'), may hold values from -6 to 6
- pseudo_grads: float32 [4, 64, 1024], P('replica', 'fsdp', 'tensor'), may hold values from -6 to 6
- outer_params: float32 [40, 64, 1024], P(None, ('fsdp', 'replica'), 'tensor'), may hold values from -6 to 6
- outer_moment: float32 [40, 64, 1024], P(None, ('fsdp', 'replica'), 'tensor'), may hold values from -6 to 6
- token_counts: int32 [4], replicated, may hold values from 4096 to 16383
- due_index: int32 [1], replicated, may hold values from 0 to 39
Outputs:
- keys: bfloat16 [1024, 1024], P(('replica', 'fsdp'), 'tensor')
- key_weight_grad: bfloat16 [4, 8192, 1024], P('replica', 'fsdp', 'tensor')
- hidden_grad: bfloat16 [1024, 8192], P(('replica', 'fsdp'), 'tensor')
- fresh_params: bfloat16 [64, 1024], P('fsdp', 'tensor')
- fresh_moment: float32 [64, 1024], P(('fsdp', 'replica'), 'tensor')
The draws below stay inside these ranges and needn't reach their ends.
All inputs are finite; a program needn't handle non-finite values.
Results may differ from the reference program's by a relative error of at most 0.009.
Values may be sent and summed in bfloat16 or wider, within the bound.
No kernel may reach another device: no remote copies, remote signals or barrier semaphores. Data moves between devices by JAX's collectives and lax.ppermute only.
A program may use at most 64 MiB of HBM per device.

```python
import jax
import jax.numpy as jnp
from jax import lax

D = 8192
KV = 1024
TOK_DEV = 128
NFRAG = 40
TOKENS = 1024
FRAG_ROWS = 64
N_REPLICA = 4
N_FSDP = 2
N_TENSOR = 4


def set_ends(result, own_key, smallest, largest):
    place = [jax.random.randint(jax.random.fold_in(own_key, axis), (), 0, length) for axis, length in enumerate(result.shape)]
    longest = result.shape.index(max(result.shape))
    next_to = place[:longest] + [(place[longest] + 1) % result.shape[longest]] + place[longest + 1:]
    return result.at[tuple(place)].set(smallest).at[tuple(next_to)].set(largest)


def strengthened(result, key, source, target, blocks, factor):
    owner, partner = [(jnp.arange(result.shape[dim]) // (result.shape[dim] // blocks)).reshape([-1 if axis == dim else 1 for axis in range(result.ndim)]) for dim in (source, target)]
    chosen = jax.random.permutation(key, blocks)[partner]
    strong = (owner == chosen) | (owner == (partner + blocks // 2) % blocks)
    return jnp.where(strong, factor * result, result)


def block_levels(key, shape, shards, low, high):
    def one(position, parts):
        heights = jax.random.uniform(jax.random.fold_in(jax.random.fold_in(key, 6), position), (parts,), jnp.float32, low / len(shards), high / len(shards))
        return jnp.repeat(jnp.exp(heights), shape[position] // parts).reshape((-1,) + (1,) * (len(shape) - position - 1))

    gain = one(*shards[0])
    for cut in shards[1:]:
        gain = gain * one(*cut)
    return gain


def gaussian(own_key, shape, scale, bound, split=(), kind=jnp.bfloat16):
    drawn = jax.random.normal(own_key, shape, jnp.float32) * scale
    if len(split) > 0:
        drawn = block_levels(own_key, shape, split, -0.22, 0.18) * drawn
    return jnp.clip(drawn, min=-bound, max=bound).astype(kind)


def bell_draw_with(stream_key, extent, width, reach, shards, heavy, kind=jnp.bfloat16):
    drawn = width * jax.random.normal(stream_key, extent, jnp.float32)
    if shards:
        drawn = drawn * block_levels(stream_key, extent, shards, -0.22, 0.18)
    return jnp.clip(strengthened(drawn, jax.random.fold_in(stream_key, 3), *heavy), -reach, reach).astype(kind)


def setup_inputs(seed: int = 0) -> dict:
    splits = jax.random.split(jax.random.key(seed), 9)
    hidden = gaussian(splits[0], (TOKENS, D), 1.0, 6.0, ((0, 8),))
    key_weight = gaussian(splits[1], (N_REPLICA, D, KV), D ** -0.5, 0.0625, ((0, 4), (1, 2), (2, 4)))
    key_grad = gaussian(splits[2], (TOKENS, KV), (8 / (TOK_DEV * N_FSDP) ** 0.5), 6.0, ((0, 8), (1, 4)))
    pseudo_grads = bell_draw_with(splits[3], (N_REPLICA, FRAG_ROWS, KV), 1.0, 6.0, ((0, 4), (1, 2), (2, 4)), (0, 1, 4, 2.0), jnp.float32)
    outer_params = gaussian(splits[4], (NFRAG, FRAG_ROWS, KV), 1.0, 6.0, ((1, 8), (2, 4)), jnp.float32)
    outer_moment = gaussian(splits[5], (NFRAG, FRAG_ROWS, KV), 0.5, 6.0, ((1, 8), (2, 4)), jnp.float32)
    token_counts = set_ends(jax.random.randint(splits[6], (N_REPLICA,), 16 * TOK_DEV * N_FSDP, 64 * TOK_DEV * N_FSDP), jax.random.fold_in(splits[6], 1), 16 * TOK_DEV * N_FSDP, (64 * TOK_DEV * N_FSDP) - 1).astype(jnp.int32)
    due_index = jax.random.randint(splits[7], (1,), 0, NFRAG).astype(jnp.int32)
    return dict(hidden=hidden, key_weight=key_weight, key_grad=key_grad, pseudo_grads=pseudo_grads, outer_params=outer_params, outer_moment=outer_moment, token_counts=token_counts, due_index=due_index)


outer_rate = 0.7
momentum_rate = 0.9


def replica_step(inputs):
    tokens, weight, cotangent = inputs
    head_cols = KV // N_TENSOR
    key_values = jnp.dot(tokens, weight, preferred_element_type=jnp.float32).astype(jnp.bfloat16)
    token_groups = tokens.reshape(N_FSDP, TOK_DEV, D).astype(jnp.float32)
    cot_groups = cotangent.reshape(N_FSDP, TOK_DEV, KV).astype(jnp.float32)
    group_term = jnp.einsum("gtd,gth->gdh", token_groups, cot_groups)
    group_term = lax.optimization_barrier(group_term.astype(jnp.bfloat16))
    weight_grad = jnp.sum(group_term.astype(jnp.float32), axis=0).astype(jnp.bfloat16)
    cot_heads = cotangent.reshape(N_FSDP * TOK_DEV, N_TENSOR, head_cols).astype(jnp.float32)
    weight_heads = weight.reshape(D, N_TENSOR, head_cols).astype(jnp.float32)
    head_term = jnp.einsum("snh,dnh->nsd", cot_heads, weight_heads)
    head_term = lax.optimization_barrier(head_term.astype(jnp.bfloat16))
    input_grad = jnp.sum(head_term.astype(jnp.float32), axis=0).astype(jnp.bfloat16)
    return key_values, weight_grad, input_grad


def reference(hidden, key_weight, key_grad, pseudo_grads, outer_params, outer_moment, token_counts, due_index):
    replica_rows = TOK_DEV * N_FSDP
    stacked = (hidden.reshape(N_REPLICA, replica_rows, D), key_weight, key_grad.reshape(N_REPLICA, replica_rows, KV))
    key_values, weight_grad, input_grad = lax.map(replica_step, stacked)
    keys = key_values.reshape(N_REPLICA * replica_rows, KV)
    hidden_grad = input_grad.reshape(N_REPLICA * replica_rows, D)
    counts = token_counts.astype(jnp.float32)
    weight_share = counts / jnp.sum(counts)
    average = jnp.tensordot(weight_share, pseudo_grads, axes=1, precision=lax.Precision.HIGHEST)
    due_slot = due_index[0]
    params_now = lax.dynamic_index_in_dim(outer_params, due_slot, 0, keepdims=False)
    moment_now = lax.dynamic_index_in_dim(outer_moment, due_slot, 0, keepdims=False)
    fresh_moment = momentum_rate * moment_now + average
    fresh_params = (params_now - outer_rate * (average + momentum_rate * fresh_moment)).astype(jnp.bfloat16)
    return (keys, weight_grad, hidden_grad, fresh_params, fresh_moment)
```

```python
import jax
import jax.numpy as jnp
from jax import lax
from jax.sharding import PartitionSpec as P

outer_rate = 0.7
momentum_rate = 0.9
CHUNKS = 2


def matmul_t(a, b):
    return lax.dot_general(a, b, (((1,), (1,)), ((), ())), preferred_element_type=jnp.float32)


def flip(value, axis, bit):
    size = lax.axis_size(axis)
    return lax.ppermute(value, axis, [(i, i ^ bit) for i in range(size)])


def share_of(token_counts):
    counts = token_counts.astype(jnp.float32)
    replica_slot = lax.axis_index("replica")
    own_count = jnp.sum(jnp.where(jnp.arange(counts.shape[0]) == replica_slot, counts, 0.0))
    return own_count / jnp.sum(counts)


def outer_update(average, outer_params, outer_moment, due_index):
    due_slot = due_index[0]
    params_now = lax.dynamic_index_in_dim(outer_params, due_slot, 0, keepdims=False)
    moment_now = lax.dynamic_index_in_dim(outer_moment, due_slot, 0, keepdims=False)
    moment_new = momentum_rate * moment_now + average
    updated = params_now - outer_rate * (average + momentum_rate * moment_new)
    return updated.astype(jnp.bfloat16), moment_new


def halving_sum(value, axis):
    size = lax.axis_size(axis)
    slot = lax.axis_index(axis)
    bit = 1
    value = value.reshape(size, -1, value.shape[-1])
    while bit < size:
        mine = (slot // bit) % 2
        pairs = value.reshape(-1, 2, *value.shape[1:])
        sent = lax.dynamic_index_in_dim(pairs, 1 - mine, 1, keepdims=False)
        kept = lax.dynamic_index_in_dim(pairs, mine, 1, keepdims=False)
        value = kept + flip(sent, axis, bit)
        bit *= 2
    return value[0]


def doubling_gather(value, axis):
    size = lax.axis_size(axis)
    slot = lax.axis_index(axis)
    bit = size // 2
    value = value[None]
    while bit >= 1:
        mine = (slot // bit) % 2
        other = flip(value, axis, bit)
        low = jnp.where(mine == 0, value, other)
        high = jnp.where(mine == 0, other, value)
        value = jnp.stack([low, high], axis=1).reshape(-1, *value.shape[1:])
        bit //= 2
    return value.reshape(-1, value.shape[-1])


def on_device(
    hidden, key_weight, key_grad, pseudo_grads, outer_params, outer_moment, token_counts, due_index
):
    weight = key_weight[0]
    shard_rows = weight.shape[0]
    row_slot = lax.axis_index("fsdp")
    head_slot = lax.axis_index("tensor")
    other_cot = flip(key_grad, "fsdp", 1)
    hidden_own = lax.dynamic_slice_in_dim(hidden, row_slot * shard_rows, shard_rows, 1)
    hidden_sent = lax.dynamic_slice_in_dim(hidden, (1 - row_slot) * shard_rows, shard_rows, 1)
    half = shard_rows // 2
    moved = jnp.concatenate(
        [flip(hidden_sent[:, i * half : (i + 1) * half], "fsdp", 1) for i in range(2)], axis=1
    )
    cots = jnp.concatenate([key_grad, other_cot], axis=0)
    tok_rows = key_grad.shape[0]

    block = shard_rows // 2
    parity = head_slot % 2
    chunk = block // CHUNKS
    at_home = row_slot == head_slot // 2
    grads = []
    for c in range(CHUNKS):
        rows_sent = lax.dynamic_slice_in_dim(weight, (1 - parity) * block + c * chunk, chunk, 0)
        rows_kept = lax.dynamic_slice_in_dim(weight, parity * block + c * chunk, chunk, 0)
        sent = matmul_t(cots, rows_sent).astype(jnp.bfloat16)
        got = flip(sent, "tensor", 1).astype(jnp.float32)
        kept = matmul_t(cots, rows_kept) + got
        mine, others = kept[:tok_rows], kept[tok_rows:]
        crossed = flip(others.astype(jnp.bfloat16), "fsdp", 1)
        mine = mine.astype(jnp.bfloat16)
        away = jnp.where(at_home, crossed, mine)
        stay = jnp.where(at_home, mine, crossed)
        last = flip(away, "tensor", 2)
        grads.append((stay.astype(jnp.float32) + last.astype(jnp.float32)).astype(jnp.bfloat16))
    hidden_grad = jnp.concatenate(grads, axis=1)

    part_other = jnp.dot(moved, weight, preferred_element_type=jnp.float32).astype(jnp.bfloat16)
    part_back = flip(part_other, "fsdp", 1).astype(jnp.float32)
    keys = (jnp.dot(hidden_own, weight, preferred_element_type=jnp.float32) + part_back).astype(jnp.bfloat16)

    contract = (((0,), (0,)), ((), ()))
    weight_sum = lax.dot_general(
        jnp.concatenate([hidden_own, moved], axis=0), cots, contract, preferred_element_type=jnp.float32
    )
    weight_grad = weight_sum.astype(jnp.bfloat16)[None]

    average = halving_sum(pseudo_grads[0] * share_of(token_counts), "replica")
    updated, moment_new = outer_update(average, outer_params, outer_moment, due_index)
    gathered = doubling_gather(updated, "replica")
    return (keys, weight_grad, hidden_grad, gathered, moment_new)


def on_device_any(
    hidden, key_weight, key_grad, pseudo_grads, outer_params, outer_moment, token_counts, due_index
):
    weight = key_weight[0]
    groups = lax.axis_size("fsdp")
    tok_rows, shard_rows, head_cols = hidden.shape[0], weight.shape[0], weight.shape[1]
    block_rows = lax.all_gather(weight, "fsdp", axis=0, tiled=True)
    keys = jnp.dot(hidden, block_rows, preferred_element_type=jnp.float32).astype(jnp.bfloat16)
    input_part = matmul_t(key_grad, block_rows).astype(jnp.bfloat16)
    moved = lax.all_to_all(hidden, "fsdp", split_axis=1, concat_axis=0, tiled=True)
    cot_all = lax.all_gather(key_grad, "fsdp", axis=0, tiled=True)
    weight_sum = lax.dot_general(
        moved, cot_all, (((0,), (0,)), ((), ())), preferred_element_type=jnp.float32
    )
    weight_grad = weight_sum.astype(jnp.bfloat16)[None]
    hidden_grad = lax.psum_scatter(input_part, "tensor", scatter_dimension=1, tiled=True)
    average = lax.psum_scatter(
        pseudo_grads[0] * share_of(token_counts), "replica", scatter_dimension=0, tiled=True
    )
    updated, moment_new = outer_update(average, outer_params, outer_moment, due_index)
    gathered = lax.all_gather(updated, "replica", axis=0, tiled=True)
    return (keys, weight_grad, hidden_grad, gathered, moment_new)


def solution(mesh):
    sizes = mesh.shape
    replicas = sizes["replica"]
    fits = sizes["fsdp"] == 2 and sizes["tensor"] == 4 and replicas & (replicas - 1) == 0
    return jax.shard_map(
        on_device if fits else on_device_any,
        mesh=mesh,
        in_specs=(
            P(("replica", "fsdp"), None),
            P("replica", "fsdp", "tensor"),
            P(("replica", "fsdp"), "tensor"),
            P("replica", "fsdp", "tensor"),
            P(None, ("fsdp", "replica"), "tensor"),
            P(None, ("fsdp", "replica"), "tensor"),
            P(),
            P(),
        ),
        out_specs=(
            P(("replica", "fsdp"), "tensor"),
            P("replica", "fsdp", "tensor"),
            P(("replica", "fsdp"), "tensor"),
            P("fsdp", "tensor"),
            P(("fsdp", "replica"), "tensor"),
        ),
        check_vma=False,
    )
```

```python
import functools
import math

import jax
import jax.numpy as jnp
from jax import lax
from jax.experimental import pallas as pl
from jax.experimental.pallas import tpu as pltpu
from jax.sharding import PartitionSpec as P

outer_rate = 0.7
momentum_rate = 0.9
PARTS = (6, 6, 4)
LOAD_LIMIT = 50
GRADS = ((0, 1), (2,))
FINALS = ((0, 1), (2,))
PIECES = (3, 3, 2)


def matmul_t(a, b):
    return lax.dot_general(a, b, (((1,), (1,)), ((), ())), preferred_element_type=jnp.float32)


def matmul_first(a, b):
    return lax.dot_general(a, b, (((0,), (0,)), ((), ())), preferred_element_type=jnp.float32)


def flip(value, axis, bit):
    size = lax.axis_size(axis)
    return lax.ppermute(value, axis, [(i, i ^ bit) for i in range(size)])


def share_of(token_counts):
    counts = token_counts.astype(jnp.float32)
    replica_slot = lax.axis_index("replica")
    own_count = jnp.sum(jnp.where(jnp.arange(counts.shape[0]) == replica_slot, counts, 0.0))
    return own_count / jnp.sum(counts)


def stepped(average, params_now, moment_now):
    moment_new = momentum_rate * moment_now + average
    updated = params_now - outer_rate * (average + momentum_rate * moment_new)
    return updated.astype(jnp.bfloat16), moment_new


def due_rows(outer_params, outer_moment, due_index):
    due_slot = due_index[0]
    params_now = lax.dynamic_index_in_dim(outer_params, due_slot, 0, keepdims=False)
    moment_now = lax.dynamic_index_in_dim(outer_moment, due_slot, 0, keepdims=False)
    return params_now, moment_now


VMEM = pl.BlockSpec(memory_space=pltpu.VMEM)
HBM = pl.BlockSpec(memory_space=pltpu.HBM)
SMEM = pl.BlockSpec(memory_space=pltpu.SMEM)


def call(kernel, out_shape, in_specs, out_specs, scratch=(), aliases=None, flops=0, limit=10):
    def run(*arrays):
        return pl.pallas_call(
            kernel,
            out_shape=out_shape,
            in_specs=in_specs,
            out_specs=out_specs,
            scratch_shapes=scratch,
            input_output_aliases=aliases or {},
            compiler_params=pltpu.CompilerParams(vmem_limit_bytes=limit * 2**20),
            cost_estimate=pl.CostEstimate(flops=flops, bytes_accessed=2**20, transcendentals=0),
        )(*arrays)

    return run


def load_kernel(hidden, weight, sent, weight_out, sems):
    start = pl.multiple_of((1 - lax.axis_index("fsdp")) * weight.shape[0], 128)
    copies = [
        pltpu.make_async_copy(hidden.at[:, pl.ds(start, sent.shape[1])], sent, sems.at[0]),
        pltpu.make_async_copy(weight, weight_out, sems.at[1]),
    ]
    for copy in copies:
        copy.start()
    for copy in copies:
        copy.wait()


def late_load_kernel(rows, base, hidden, sent, sem):
    start = pl.multiple_of((1 - lax.axis_index("fsdp")) * rows + base, 128)
    copy = pltpu.make_async_copy(hidden.at[:, pl.ds(start, sent.shape[1])], sent, sem)
    copy.start()
    copy.wait()


def sent_kernel(weight, own, other, *outs):
    block = sum(out.shape[1] for out in outs) // 2
    offset = (1 - lax.axis_index("tensor") % 2) * block
    for i, out in enumerate(outs):
        if i == len(outs) // 2:
            offset = offset - block
        rows = weight[pl.ds(pl.multiple_of(offset, 128), out.shape[1]), :]
        out[...] = matmul_t((other if i < len(outs) // 2 else own)[...], rows).astype(out.dtype)
        offset = offset + out.shape[1]


def kept_kernel(weight, own, other, *outs):
    tokens = own.shape[0]
    offset = (lax.axis_index("tensor") % 2) * sum(out.shape[1] for out in outs)
    for out in outs:
        rows = weight[pl.ds(pl.multiple_of(offset, 128), out.shape[1]), :]
        out[:tokens] = matmul_t(own[...], rows)
        out[tokens:] = matmul_t(other[...], rows)
        offset = offset + out.shape[1]


def others_kernel(kept, got, out):
    out[...] = (kept[out.shape[0] :] + got[...].astype(jnp.float32)).astype(out.dtype)


def at_home(shape):
    home = (lax.axis_index("fsdp") == lax.axis_index("tensor") // 2).astype(jnp.int32)
    return jnp.full(shape, home, jnp.int32) == 1


def select_kernel(kept, got, crossed, away, stay):
    mine = (kept[: away.shape[0]] + got[...].astype(jnp.float32)).astype(away.dtype)
    home = at_home(away.shape)
    away[...] = jnp.where(home, crossed[...], mine)
    stay[...] = jnp.where(home, mine, crossed[...])


def final_parts(base, parts, out, made, sems):
    copies, offset = [], 0
    for i in range(len(parts) // 2):
        stay, last = parts[2 * i : 2 * i + 2]
        columns = pl.ds(offset, stay.shape[1])
        total = stay[...].astype(jnp.float32) + last[...].astype(jnp.float32)
        made[:, columns] = total.astype(made.dtype)
        where = pl.ds(base + offset, stay.shape[1])
        copies.append(pltpu.make_async_copy(made.at[:, columns], out.at[:, where], sems.at[i]))
        copies[i].start()
        offset += stay.shape[1]
    return copies


def final_kernel(base, count, *refs):
    for copy in final_parts(base, refs[: 2 * count], *refs[-3:]):
        copy.wait()


def last_kernel(base, count, *refs):
    parts, (own_part, back, packed, got) = refs[: 2 * count], refs[2 * count : 2 * count + 4]
    out, keys, params_out, moment_out, made, sems = refs[-6:]
    copies = final_parts(base, parts, out, made, sems)
    keys[...] = (own_part[...] + back[...].astype(jnp.float32)).astype(keys.dtype)
    outer_last(params_out.shape[0], moment_out.shape[0], packed, got, params_out, moment_out)
    for copy in copies:
        copy.wait()


def weights_kernel(base, width, count, hidden, own_cot, other_cot, *rest):
    moved, (out, left, made, sems) = rest[:count], rest[-4:]
    start = pl.multiple_of(lax.axis_index("fsdp") * out.shape[0] + base, 128)
    blocks = [(piece, at) for piece in moved for at in range(0, piece.shape[1], width)]
    reads, writes = [], []
    for b in range(len(blocks)):
        columns = pl.ds(start + b * width, width)
        reads.append(pltpu.make_async_copy(hidden.at[:, columns], left.at[b], sems.at[0, b]))
        reads[b].start()
    for b, (piece, at) in enumerate(blocks):
        reads[b].wait()
        right = piece[:, at : at + width]
        total = matmul_first(left[b], own_cot[...]) + matmul_first(right, other_cot[...])
        made[b] = total.astype(made.dtype)
        writes.append(
            pltpu.make_async_copy(made.at[b], out.at[pl.ds(base + b * width, width)], sems.at[1, b])
        )
        writes[b].start()
    for copy in writes:
        copy.wait()


def weight_rows(hidden, moved, own_cot, other_cot, rows, base, before):
    tokens, head_cols = own_cot.shape
    columns = sum(piece.shape[1] for piece in moved)
    width = math.gcd(512, *(piece.shape[1] for piece in moved))
    blocks = columns // width
    kept = () if before is None else (before,)
    run = call(
        functools.partial(weights_kernel, base, width, len(moved)),
        jax.ShapeDtypeStruct((rows, head_cols), jnp.bfloat16),
        [HBM] + [VMEM] * (2 + len(moved)) + [HBM] * len(kept),
        HBM,
        [
            pltpu.VMEM((blocks, tokens, width), hidden.dtype),
            pltpu.VMEM((blocks, width, head_cols), jnp.bfloat16),
            pltpu.SemaphoreType.DMA((2, blocks)),
        ],
        {3 + len(moved): 0} if kept else {},
        4 * tokens * head_cols * columns,
    )
    return run(hidden, own_cot, other_cot, *moved, *kept)


def keys_own_kernel(hidden, moved, weight, own_part, moved_part, left, sem):
    start = pl.multiple_of(lax.axis_index("fsdp") * weight.shape[0], 128)
    copy = pltpu.make_async_copy(hidden.at[:, pl.ds(start, left.shape[1])], left, sem)
    copy.start()
    half = moved.shape[1]
    moved_part[...] = jnp.dot(moved[...], weight[:half], preferred_element_type=jnp.float32)
    copy.wait()
    own_part[...] = jnp.dot(left[...], weight[...], preferred_element_type=jnp.float32)


def keys_sent_kernel(part, weight, *rest):
    moved, out = rest[:-1], rest[-1]
    total = part[...]
    base = weight.shape[0] - sum(piece.shape[1] for piece in moved)
    for piece in moved:
        rows = weight[base : base + piece.shape[1]]
        total = total + jnp.dot(piece[...], rows, preferred_element_type=jnp.float32)
        base += piece.shape[1]
    out[...] = total.astype(out.dtype)


def outer_first_kernel(due_index, counts, grads, params, moment, packed, sems):
    rows, own = grads.shape[0], params.shape[1]
    due, slot = due_index[0], lax.axis_index("replica")
    reads = [
        pltpu.make_async_copy(source.at[due], packed.at[pl.ds(rows + i * own, own)], sems.at[i])
        for i, source in enumerate((params, moment))
    ]
    for copy in reads:
        copy.start()
    total = jnp.float32(0)
    for i in range(counts.shape[0]):
        total = total + counts[i].astype(jnp.float32)
    shape = (1, grads.shape[1])
    share = jnp.full(shape, counts[slot].astype(jnp.float32)) / jnp.full(shape, total)
    packed[:rows] = grads[...] * share
    for copy in reads:
        copy.wait()


def lower_half(bit, shape):
    mine = (lax.axis_index("replica") // bit) % 2
    return jnp.full(shape, mine, jnp.int32) == 0


def outer_join_kernel(rows, packed, got, out):
    held = packed.shape[0] - rows
    out[:rows] = packed[:rows] + got[:rows]
    here = lower_half(1, (held, packed.shape[1]))
    out[rows : rows + held] = jnp.where(here, packed[rows:], got[rows:])
    out[rows + held :] = jnp.where(here, got[rows:], packed[rows:])


def outer_last(rows, own, packed, got, params_out, moment_out):
    average = packed[:rows] + got[:rows]
    owners = rows // own
    here = lower_half(2, (2 * own, packed.shape[1]))
    for i in range(owners):
        low = i < owners // 2
        base = rows + (i % (owners // 2)) * 2 * own
        ours, theirs = packed[base : base + 2 * own], got[base : base + 2 * own]
        held = jnp.where(here, ours, theirs) if low else jnp.where(here, theirs, ours)
        part = average[i * own : (i + 1) * own]
        updated, moment_new = stepped(part, held[:own], held[own:])
        params_out[i * own : (i + 1) * own] = updated

        @pl.when(lax.axis_index("replica") == i)
        def _():
            moment_out[...] = moment_new


def outer_step(pseudo_grads, outer_params, outer_moment, token_counts, due_index):
    grads = pseudo_grads[0]
    rows, columns = grads.shape
    own = outer_params.shape[1]

    def packed_shape(owners):
        return jax.ShapeDtypeStruct((rows + 2 * own * owners, columns), jnp.float32)

    specs = [SMEM, SMEM, VMEM, HBM, HBM]
    sems = [pltpu.SemaphoreType.DMA((2,))]
    packed = call(outer_first_kernel, packed_shape(1), specs, VMEM, sems)(
        due_index, token_counts, grads, outer_params, outer_moment
    )
    got = flip(packed, "replica", 1)
    kernel = functools.partial(outer_join_kernel, rows)
    packed = call(kernel, packed_shape(2), [VMEM, VMEM], VMEM)(packed, got)
    got = flip(packed, "replica", 2)
    outs = (
        jax.ShapeDtypeStruct((rows, columns), jnp.bfloat16),
        jax.ShapeDtypeStruct((own, columns), jnp.float32),
    )
    return packed, got, outs


def on_device(
    hidden, key_weight, key_grad, pseudo_grads, outer_params, outer_moment, token_counts, due_index
):
    shard_rows, head_cols = key_weight.shape[1:]
    tok_rows = key_grad.shape[0]
    widths = [shard_rows * piece // sum(PIECES) for piece in PIECES]
    bases = [sum(widths[:i]) for i in range(len(widths))]
    other_cot = flip(key_grad, "fsdp", 1)
    narrow = jax.ShapeDtypeStruct((tok_rows, widths[0]), hidden.dtype)
    outs = (narrow, jax.ShapeDtypeStruct((shard_rows, head_cols), key_weight.dtype))
    sems = [pltpu.SemaphoreType.DMA((2,))]
    sent, weight = call(load_kernel, outs, [HBM] * 2, (VMEM,) * 2, sems, limit=LOAD_LIMIT)(
        hidden, key_weight[0]
    )
    moved = [flip(sent, "fsdp", 1)]
    for i in range(1, len(widths)):
        narrow = jax.ShapeDtypeStruct((tok_rows, widths[i]), hidden.dtype)
        kernel = functools.partial(late_load_kernel, shard_rows, bases[i])
        sent = call(kernel, narrow, [HBM], VMEM, [pltpu.SemaphoreType.DMA])(hidden)
        moved.append(flip(sent, "fsdp", 1))

    block = shard_rows // 2
    chunks = [block * part // sum(PARTS) for part in PARTS]
    count, flops = len(chunks), 4 * tok_rows * head_cols * block
    part = [jax.ShapeDtypeStruct((tok_rows, chunk), jnp.bfloat16) for chunk in chunks]
    both = [jax.ShapeDtypeStruct((2 * tok_rows, chunk), jnp.float32) for chunk in chunks]
    inputs = (weight, key_grad, other_cot)
    gone = call(sent_kernel, part * 2, [VMEM] * 3, [VMEM] * (2 * count), flops=flops)(*inputs)
    kept = call(kept_kernel, both, [VMEM] * 3, [VMEM] * count, flops=flops)(*inputs)
    got = [flip(gone[c], "tensor", 1) for c in range(count)]
    got_own = [flip(gone[count + c], "tensor", 1) for c in range(count)]
    ends = []
    for c in range(count):
        others = call(others_kernel, part[c], [VMEM] * 2, VMEM)(kept[c], got[c])
        crossed = flip(others, "fsdp", 1)
        run = call(select_kernel, (part[c],) * 2, [VMEM] * 3, (VMEM,) * 2)
        away, stay = run(kept[c], got_own[c], crossed)
        ends.append((stay, flip(away, "tensor", 2)))
    sums = jax.ShapeDtypeStruct((tok_rows, head_cols), jnp.float32)
    own_part, moved_part = call(
        keys_own_kernel,
        (sums, sums),
        [HBM, VMEM, VMEM],
        (VMEM, VMEM),
        [pltpu.VMEM((tok_rows, shard_rows), hidden.dtype), pltpu.SemaphoreType.DMA],
    )(hidden, moved[0], weight)
    part = jax.ShapeDtypeStruct((tok_rows, head_cols), jnp.bfloat16)
    sums_sent = call(keys_sent_kernel, part, [VMEM] * (1 + len(moved)), VMEM)(
        moved_part, weight, *moved[1:]
    )
    back = flip(sums_sent, "fsdp", 1)

    weight_grad = None
    for group in GRADS:
        pieces = [moved[p] for p in group]
        weight_grad = weight_rows(
            hidden, pieces, key_grad, other_cot, shard_rows, bases[group[0]], weight_grad
        )

    outer, outer_got, outer_outs = outer_step(
        pseudo_grads, outer_params, outer_moment, token_counts, due_index
    )

    hidden_grad, base = None, 0
    for i, group in enumerate(FINALS):
        ending = i == len(FINALS) - 1
        before = () if hidden_grad is None else (hidden_grad,)
        parts = [array for c in group for array in ends[c]]
        width = sum(chunks[c] for c in group)
        extra = (own_part, back, outer, outer_got) if ending else ()
        outs = (jax.ShapeDtypeStruct((tok_rows, block), jnp.bfloat16),)
        kernel = functools.partial(final_kernel, base, len(group))
        if ending:
            outs += (part, *outer_outs)
            kernel = functools.partial(last_kernel, base, len(group))
        run = call(
            kernel,
            outs,
            [VMEM] * (len(parts) + len(extra)) + [HBM] * len(before),
            (HBM,) + (VMEM,) * (len(outs) - 1),
            [pltpu.VMEM((tok_rows, width), jnp.bfloat16), pltpu.SemaphoreType.DMA((len(group),))],
            {len(parts) + len(extra): 0} if before else {},
        )
        hidden_grad, *others = run(*parts, *extra, *before)
        base += width
    keys, fresh_params, fresh_moment = others
    return (keys, weight_grad[None], hidden_grad, fresh_params, fresh_moment)


def on_device_any(
    hidden, key_weight, key_grad, pseudo_grads, outer_params, outer_moment, token_counts, due_index
):
    weight = key_weight[0]
    block_rows = lax.all_gather(weight, "fsdp", axis=0, tiled=True)
    keys = jnp.dot(hidden, block_rows, preferred_element_type=jnp.float32).astype(jnp.bfloat16)
    input_part = matmul_t(key_grad, block_rows).astype(jnp.bfloat16)
    moved = lax.all_to_all(hidden, "fsdp", split_axis=1, concat_axis=0, tiled=True)
    cot_all = lax.all_gather(key_grad, "fsdp", axis=0, tiled=True)
    weight_grad = matmul_first(moved, cot_all).astype(jnp.bfloat16)[None]
    hidden_grad = lax.psum_scatter(input_part, "tensor", scatter_dimension=1, tiled=True)
    average = lax.psum_scatter(
        pseudo_grads[0] * share_of(token_counts), "replica", scatter_dimension=0, tiled=True
    )
    updated, moment_new = stepped(average, *due_rows(outer_params, outer_moment, due_index))
    gathered = lax.all_gather(updated, "replica", axis=0, tiled=True)
    return (keys, weight_grad, hidden_grad, gathered, moment_new)


def solution(mesh):
    sizes = mesh.shape
    fits = sizes["fsdp"] == 2 and sizes["tensor"] == 4 and sizes["replica"] == 4

    def step(*arrays):
        return (on_device if fits else on_device_any)(*arrays)

    return jax.shard_map(
        step,
        mesh=mesh,
        in_specs=(
            P(("replica", "fsdp"), None),
            P("replica", "fsdp", "tensor"),
            P(("replica", "fsdp"), "tensor"),
            P("replica", "fsdp", "tensor"),
            P(None, ("fsdp", "replica"), "tensor"),
            P(None, ("fsdp", "replica"), "tensor"),
            P(),
            P(),
        ),
        out_specs=(
            P(("replica", "fsdp"), "tensor"),
            P("replica", "fsdp", "tensor"),
            P(("replica", "fsdp"), "tensor"),
            P("fsdp", "tensor"),
            P(("fsdp", "replica"), "tensor"),
        ),
        check_vma=False,
    )
```

```python
import functools
import math

import jax
import jax.numpy as jnp
from jax import lax
from jax.experimental import pallas as pl
from jax.experimental.pallas import tpu as pltpu
from jax.sharding import PartitionSpec as P

outer_rate = 0.7
momentum_rate = 0.9
PARTS = (4, 7, 5)
LOAD_LIMIT = 50
GRADS = ((0,), (1, 2))
FINALS = ((0, 1), (2,))
PIECES = (4, 3, 1)


def matmul_t(a, b):
    return lax.dot_general(a, b, (((1,), (1,)), ((), ())), preferred_element_type=jnp.float32)


def matmul_first(a, b):
    return lax.dot_general(a, b, (((0,), (0,)), ((), ())), preferred_element_type=jnp.float32)


def flip(value, axis, bit):
    size = lax.axis_size(axis)
    return lax.ppermute(value, axis, [(i, i ^ bit) for i in range(size)])


def share_of(token_counts):
    counts = token_counts.astype(jnp.float32)
    replica_slot = lax.axis_index("replica")
    own_count = jnp.sum(jnp.where(jnp.arange(counts.shape[0]) == replica_slot, counts, 0.0))
    return own_count / jnp.sum(counts)


def stepped(average, params_now, moment_now):
    moment_new = momentum_rate * moment_now + average
    updated = params_now - outer_rate * (average + momentum_rate * moment_new)
    return updated.astype(jnp.bfloat16), moment_new


def due_rows(outer_params, outer_moment, due_index):
    due_slot = due_index[0]
    params_now = lax.dynamic_index_in_dim(outer_params, due_slot, 0, keepdims=False)
    moment_now = lax.dynamic_index_in_dim(outer_moment, due_slot, 0, keepdims=False)
    return params_now, moment_now


VMEM = pl.BlockSpec(memory_space=pltpu.VMEM)
HBM = pl.BlockSpec(memory_space=pltpu.HBM)
SMEM = pl.BlockSpec(memory_space=pltpu.SMEM)


def call(kernel, out_shape, in_specs, out_specs, scratch=(), aliases=None, flops=0, limit=10):
    def run(*arrays):
        return pl.pallas_call(
            kernel,
            out_shape=out_shape,
            in_specs=in_specs,
            out_specs=out_specs,
            scratch_shapes=scratch,
            input_output_aliases=aliases or {},
            compiler_params=pltpu.CompilerParams(vmem_limit_bytes=limit * 2**20),
            cost_estimate=pl.CostEstimate(flops=flops, bytes_accessed=2**20, transcendentals=0),
        )(*arrays)

    return run


def load_kernel(hidden, weight, sent, weight_out, sems):
    start = pl.multiple_of((1 - lax.axis_index("fsdp")) * weight.shape[0], 128)
    copies = [
        pltpu.make_async_copy(hidden.at[:, pl.ds(start, sent.shape[1])], sent, sems.at[0]),
        pltpu.make_async_copy(weight, weight_out, sems.at[1]),
    ]
    for copy in copies:
        copy.start()
    for copy in copies:
        copy.wait()


def late_load_kernel(rows, base, hidden, sent, sem):
    start = pl.multiple_of((1 - lax.axis_index("fsdp")) * rows + base, 128)
    copy = pltpu.make_async_copy(hidden.at[:, pl.ds(start, sent.shape[1])], sent, sem)
    copy.start()
    copy.wait()


def sent_kernel(weight, cot, *outs):
    offset = (1 - lax.axis_index("tensor") % 2) * sum(out.shape[1] for out in outs)
    for out in outs:
        rows = weight[pl.ds(pl.multiple_of(offset, 128), out.shape[1]), :]
        out[...] = matmul_t(cot[...], rows).astype(out.dtype)
        offset = offset + out.shape[1]


def kept_kernel(weight, own, other, *outs):
    tokens = own.shape[0]
    offset = (lax.axis_index("tensor") % 2) * sum(out.shape[1] for out in outs)
    for out in outs:
        rows = weight[pl.ds(pl.multiple_of(offset, 128), out.shape[1]), :]
        out[:tokens] = matmul_t(own[...], rows)
        out[tokens:] = matmul_t(other[...], rows)
        offset = offset + out.shape[1]


def others_kernel(kept, got, out):
    out[...] = (kept[out.shape[0] :] + got[...].astype(jnp.float32)).astype(out.dtype)


def at_home(shape):
    home = (lax.axis_index("fsdp") == lax.axis_index("tensor") // 2).astype(jnp.int32)
    return jnp.full(shape, home, jnp.int32) == 1


def select_kernel(kept, got, crossed, away, stay):
    mine = (kept[: away.shape[0]] + got[...].astype(jnp.float32)).astype(away.dtype)
    home = at_home(away.shape)
    away[...] = jnp.where(home, crossed[...], mine)
    stay[...] = jnp.where(home, mine, crossed[...])


def final_parts(base, parts, out, made, sems):
    copies, offset = [], 0
    for i in range(len(parts) // 2):
        stay, last = parts[2 * i : 2 * i + 2]
        columns = pl.ds(offset, stay.shape[1])
        total = stay[...].astype(jnp.float32) + last[...].astype(jnp.float32)
        made[:, columns] = total.astype(made.dtype)
        where = pl.ds(base + offset, stay.shape[1])
        copies.append(pltpu.make_async_copy(made.at[:, columns], out.at[:, where], sems.at[i]))
        copies[i].start()
        offset += stay.shape[1]
    return copies


def final_kernel(base, count, *refs):
    for copy in final_parts(base, refs[: 2 * count], *refs[-3:]):
        copy.wait()


def last_kernel(base, count, *refs):
    parts, (own_part, back, packed, got) = refs[: 2 * count], refs[2 * count : 2 * count + 4]
    out, keys, params_out, moment_out, made, sems = refs[-6:]
    copies = final_parts(base, parts, out, made, sems)
    keys[...] = (own_part[...] + back[...].astype(jnp.float32)).astype(keys.dtype)
    outer_last(params_out.shape[0], moment_out.shape[0], packed, got, params_out, moment_out)
    for copy in copies:
        copy.wait()


def weights_kernel(base, width, count, hidden, own_cot, other_cot, *rest):
    moved, (out, left, made, sems) = rest[:count], rest[-4:]
    start = pl.multiple_of(lax.axis_index("fsdp") * out.shape[0] + base, 128)
    blocks = [(piece, at) for piece in moved for at in range(0, piece.shape[1], width)]
    reads, writes = [], []
    for b in range(len(blocks)):
        columns = pl.ds(start + b * width, width)
        reads.append(pltpu.make_async_copy(hidden.at[:, columns], left.at[b], sems.at[0, b]))
        reads[b].start()
    for b, (piece, at) in enumerate(blocks):
        reads[b].wait()
        right = piece[:, at : at + width]
        total = matmul_first(left[b], own_cot[...]) + matmul_first(right, other_cot[...])
        made[b] = total.astype(made.dtype)
        writes.append(
            pltpu.make_async_copy(made.at[b], out.at[pl.ds(base + b * width, width)], sems.at[1, b])
        )
        writes[b].start()
    for copy in writes:
        copy.wait()


def weight_rows(hidden, moved, own_cot, other_cot, rows, base, before):
    tokens, head_cols = own_cot.shape
    columns = sum(piece.shape[1] for piece in moved)
    width = math.gcd(512, *(piece.shape[1] for piece in moved))
    blocks = columns // width
    kept = () if before is None else (before,)
    run = call(
        functools.partial(weights_kernel, base, width, len(moved)),
        jax.ShapeDtypeStruct((rows, head_cols), jnp.bfloat16),
        [HBM] + [VMEM] * (2 + len(moved)) + [HBM] * len(kept),
        HBM,
        [
            pltpu.VMEM((blocks, tokens, width), hidden.dtype),
            pltpu.VMEM((blocks, width, head_cols), jnp.bfloat16),
            pltpu.SemaphoreType.DMA((2, blocks)),
        ],
        {3 + len(moved): 0} if kept else {},
        4 * tokens * head_cols * columns,
    )
    return run(hidden, own_cot, other_cot, *moved, *kept)


def keys_own_kernel(hidden, moved, weight, own_part, moved_part, left, sem):
    start = pl.multiple_of(lax.axis_index("fsdp") * weight.shape[0], 128)
    copy = pltpu.make_async_copy(hidden.at[:, pl.ds(start, left.shape[1])], left, sem)
    copy.start()
    half = moved.shape[1]
    moved_part[...] = jnp.dot(moved[...], weight[:half], preferred_element_type=jnp.float32)
    copy.wait()
    own_part[...] = jnp.dot(left[...], weight[...], preferred_element_type=jnp.float32)


def keys_sent_kernel(part, weight, *rest):
    moved, out = rest[:-1], rest[-1]
    total = part[...]
    base = weight.shape[0] - sum(piece.shape[1] for piece in moved)
    for piece in moved:
        rows = weight[base : base + piece.shape[1]]
        total = total + jnp.dot(piece[...], rows, preferred_element_type=jnp.float32)
        base += piece.shape[1]
    out[...] = total.astype(out.dtype)


def outer_first_kernel(due_index, counts, grads, params, moment, packed, sems):
    rows, own = grads.shape[0], params.shape[1]
    due, slot = due_index[0], lax.axis_index("replica")
    reads = [
        pltpu.make_async_copy(source.at[due], packed.at[pl.ds(rows + i * own, own)], sems.at[i])
        for i, source in enumerate((params, moment))
    ]
    for copy in reads:
        copy.start()
    total = jnp.float32(0)
    for i in range(counts.shape[0]):
        total = total + counts[i].astype(jnp.float32)
    shape = (1, grads.shape[1])
    share = jnp.full(shape, counts[slot].astype(jnp.float32)) / jnp.full(shape, total)
    packed[:rows] = grads[...] * share
    for copy in reads:
        copy.wait()


def lower_half(bit, shape):
    mine = (lax.axis_index("replica") // bit) % 2
    return jnp.full(shape, mine, jnp.int32) == 0


def outer_join_kernel(rows, packed, got, out):
    held = packed.shape[0] - rows
    out[:rows] = packed[:rows] + got[:rows]
    here = lower_half(1, (held, packed.shape[1]))
    out[rows : rows + held] = jnp.where(here, packed[rows:], got[rows:])
    out[rows + held :] = jnp.where(here, got[rows:], packed[rows:])


def outer_last(rows, own, packed, got, params_out, moment_out):
    average = packed[:rows] + got[:rows]
    owners = rows // own
    here = lower_half(2, (2 * own, packed.shape[1]))
    for i in range(owners):
        low = i < owners // 2
        base = rows + (i % (owners // 2)) * 2 * own
        ours, theirs = packed[base : base + 2 * own], got[base : base + 2 * own]
        held = jnp.where(here, ours, theirs) if low else jnp.where(here, theirs, ours)
        part = average[i * own : (i + 1) * own]
        updated, moment_new = stepped(part, held[:own], held[own:])
        params_out[i * own : (i + 1) * own] = updated

        @pl.when(lax.axis_index("replica") == i)
        def _():
            moment_out[...] = moment_new


def outer_step(pseudo_grads, outer_params, outer_moment, token_counts, due_index):
    grads = pseudo_grads[0]
    rows, columns = grads.shape
    own = outer_params.shape[1]

    def packed_shape(owners):
        return jax.ShapeDtypeStruct((rows + 2 * own * owners, columns), jnp.float32)

    specs = [SMEM, SMEM, VMEM, HBM, HBM]
    sems = [pltpu.SemaphoreType.DMA((2,))]
    packed = call(outer_first_kernel, packed_shape(1), specs, VMEM, sems)(
        due_index, token_counts, grads, outer_params, outer_moment
    )
    got = flip(packed, "replica", 1)
    kernel = functools.partial(outer_join_kernel, rows)
    packed = call(kernel, packed_shape(2), [VMEM, VMEM], VMEM)(packed, got)
    got = flip(packed, "replica", 2)
    outs = (
        jax.ShapeDtypeStruct((rows, columns), jnp.bfloat16),
        jax.ShapeDtypeStruct((own, columns), jnp.float32),
    )
    return packed, got, outs


def on_device(
    hidden, key_weight, key_grad, pseudo_grads, outer_params, outer_moment, token_counts, due_index
):
    shard_rows, head_cols = key_weight.shape[1:]
    tok_rows = key_grad.shape[0]
    widths = [shard_rows * piece // sum(PIECES) for piece in PIECES]
    bases = [sum(widths[:i]) for i in range(len(widths))]
    other_cot = flip(key_grad, "fsdp", 1)
    narrow = jax.ShapeDtypeStruct((tok_rows, widths[0]), hidden.dtype)
    outs = (narrow, jax.ShapeDtypeStruct((shard_rows, head_cols), key_weight.dtype))
    sems = [pltpu.SemaphoreType.DMA((2,))]
    sent, weight = call(load_kernel, outs, [HBM] * 2, (VMEM,) * 2, sems, limit=LOAD_LIMIT)(
        hidden, key_weight[0]
    )
    moved = [flip(sent, "fsdp", 1)]
    for i in range(1, len(widths)):
        narrow = jax.ShapeDtypeStruct((tok_rows, widths[i]), hidden.dtype)
        kernel = functools.partial(late_load_kernel, shard_rows, bases[i])
        sent = call(kernel, narrow, [HBM], VMEM, [pltpu.SemaphoreType.DMA])(hidden)
        moved.append(flip(sent, "fsdp", 1))

    block = shard_rows // 2
    chunks = [block * part // sum(PARTS) for part in PARTS]
    count, flops = len(chunks), 4 * tok_rows * head_cols * block
    part = [jax.ShapeDtypeStruct((tok_rows, chunk), jnp.bfloat16) for chunk in chunks]
    both = [jax.ShapeDtypeStruct((2 * tok_rows, chunk), jnp.float32) for chunk in chunks]
    got_own, got = [
        [
            flip(gone, "tensor", 1)
            for gone in call(sent_kernel, part, [VMEM] * 2, [VMEM] * count, flops=flops)(weight, cot)
        ]
        for cot in (key_grad, other_cot)
    ]
    kept = call(kept_kernel, both, [VMEM] * 3, [VMEM] * count, flops=flops)(
        weight, key_grad, other_cot
    )
    ends = []
    for c in range(count):
        others = call(others_kernel, part[c], [VMEM] * 2, VMEM)(kept[c], got[c])
        crossed = flip(others, "fsdp", 1)
        run = call(select_kernel, (part[c],) * 2, [VMEM] * 3, (VMEM,) * 2)
        away, stay = run(kept[c], got_own[c], crossed)
        ends.append((stay, flip(away, "tensor", 2)))
    sums = jax.ShapeDtypeStruct((tok_rows, head_cols), jnp.float32)
    own_part, moved_part = call(
        keys_own_kernel,
        (sums, sums),
        [HBM, VMEM, VMEM],
        (VMEM, VMEM),
        [pltpu.VMEM((tok_rows, shard_rows), hidden.dtype), pltpu.SemaphoreType.DMA],
    )(hidden, moved[0], weight)
    part = jax.ShapeDtypeStruct((tok_rows, head_cols), jnp.bfloat16)
    sums_sent = call(keys_sent_kernel, part, [VMEM] * (1 + len(moved)), VMEM)(
        moved_part, weight, *moved[1:]
    )
    back = flip(sums_sent, "fsdp", 1)

    weight_grad = None
    for group in GRADS:
        pieces = [moved[p] for p in group]
        weight_grad = weight_rows(
            hidden, pieces, key_grad, other_cot, shard_rows, bases[group[0]], weight_grad
        )

    outer, outer_got, outer_outs = outer_step(
        pseudo_grads, outer_params, outer_moment, token_counts, due_index
    )

    hidden_grad, base = None, 0
    for i, group in enumerate(FINALS):
        ending = i == len(FINALS) - 1
        before = () if hidden_grad is None else (hidden_grad,)
        parts = [array for c in group for array in ends[c]]
        width = sum(chunks[c] for c in group)
        extra = (own_part, back, outer, outer_got) if ending else ()
        outs = (jax.ShapeDtypeStruct((tok_rows, block), jnp.bfloat16),)
        kernel = functools.partial(final_kernel, base, len(group))
        if ending:
            outs += (part, *outer_outs)
            kernel = functools.partial(last_kernel, base, len(group))
        run = call(
            kernel,
            outs,
            [VMEM] * (len(parts) + len(extra)) + [HBM] * len(before),
            (HBM,) + (VMEM,) * (len(outs) - 1),
            [pltpu.VMEM((tok_rows, width), jnp.bfloat16), pltpu.SemaphoreType.DMA((len(group),))],
            {len(parts) + len(extra): 0} if before else {},
        )
        hidden_grad, *others = run(*parts, *extra, *before)
        base += width
    keys, fresh_params, fresh_moment = others
    return (keys, weight_grad[None], hidden_grad, fresh_params, fresh_moment)


def on_device_any(
    hidden, key_weight, key_grad, pseudo_grads, outer_params, outer_moment, token_counts, due_index
):
    weight = key_weight[0]
    block_rows = lax.all_gather(weight, "fsdp", axis=0, tiled=True)
    keys = jnp.dot(hidden, block_rows, preferred_element_type=jnp.float32).astype(jnp.bfloat16)
    input_part = matmul_t(key_grad, block_rows).astype(jnp.bfloat16)
    moved = lax.all_to_all(hidden, "fsdp", split_axis=1, concat_axis=0, tiled=True)
    cot_all = lax.all_gather(key_grad, "fsdp", axis=0, tiled=True)
    weight_grad = matmul_first(moved, cot_all).astype(jnp.bfloat16)[None]
    hidden_grad = lax.psum_scatter(input_part, "tensor", scatter_dimension=1, tiled=True)
    average = lax.psum_scatter(
        pseudo_grads[0] * share_of(token_counts), "replica", scatter_dimension=0, tiled=True
    )
    updated, moment_new = stepped(average, *due_rows(outer_params, outer_moment, due_index))
    gathered = lax.all_gather(updated, "replica", axis=0, tiled=True)
    return (keys, weight_grad, hidden_grad, gathered, moment_new)


def solution(mesh):
    sizes = mesh.shape
    fits = sizes["fsdp"] == 2 and sizes["tensor"] == 4 and sizes["replica"] == 4

    def step(*arrays):
        return (on_device if fits else on_device_any)(*arrays)

    return jax.shard_map(
        step,
        mesh=mesh,
        in_specs=(
            P(("replica", "fsdp"), None),
            P("replica", "fsdp", "tensor"),
            P(("replica", "fsdp"), "tensor"),
            P("replica", "fsdp", "tensor"),
            P(None, ("fsdp", "replica"), "tensor"),
            P(None, ("fsdp", "replica"), "tensor"),
            P(),
            P(),
        ),
        out_specs=(
            P(("replica", "fsdp"), "tensor"),
            P("replica", "fsdp", "tensor"),
            P(("replica", "fsdp"), "tensor"),
            P("fsdp", "tensor"),
            P(("fsdp", "replica"), "tensor"),
        ),
        check_vma=False,
    )
```

```python
import functools
import math

import jax
import jax.numpy as jnp
from jax import lax
from jax.experimental import pallas as pl
from jax.experimental.pallas import tpu as pltpu
from jax.sharding import PartitionSpec as P

outer_rate = 0.7
momentum_rate = 0.9
PARTS = (5, 7, 4)
LOAD_LIMIT = 50
GRADS = ((0,), (1,))
FINALS = ((0, 1), (2,))
PIECES = (4, 4)


def matmul_t(a, b):
    return lax.dot_general(a, b, (((1,), (1,)), ((), ())), preferred_element_type=jnp.float32)


def matmul_first(a, b):
    return lax.dot_general(a, b, (((0,), (0,)), ((), ())), preferred_element_type=jnp.float32)


def flip(value, axis, bit):
    size = lax.axis_size(axis)
    return lax.ppermute(value, axis, [(i, i ^ bit) for i in range(size)])


def share_of(token_counts):
    counts = token_counts.astype(jnp.float32)
    replica_slot = lax.axis_index("replica")
    own_count = jnp.sum(jnp.where(jnp.arange(counts.shape[0]) == replica_slot, counts, 0.0))
    return own_count / jnp.sum(counts)


def stepped(average, params_now, moment_now):
    moment_new = momentum_rate * moment_now + average
    updated = params_now - outer_rate * (average + momentum_rate * moment_new)
    return updated.astype(jnp.bfloat16), moment_new


def due_rows(outer_params, outer_moment, due_index):
    due_slot = due_index[0]
    params_now = lax.dynamic_index_in_dim(outer_params, due_slot, 0, keepdims=False)
    moment_now = lax.dynamic_index_in_dim(outer_moment, due_slot, 0, keepdims=False)
    return params_now, moment_now


VMEM = pl.BlockSpec(memory_space=pltpu.VMEM)
HBM = pl.BlockSpec(memory_space=pltpu.HBM)
SMEM = pl.BlockSpec(memory_space=pltpu.SMEM)


def call(kernel, out_shape, in_specs, out_specs, scratch=(), aliases=None, flops=0, limit=10):
    def run(*arrays):
        return pl.pallas_call(
            kernel,
            out_shape=out_shape,
            in_specs=in_specs,
            out_specs=out_specs,
            scratch_shapes=scratch,
            input_output_aliases=aliases or {},
            compiler_params=pltpu.CompilerParams(vmem_limit_bytes=limit * 2**20),
            cost_estimate=pl.CostEstimate(flops=flops, bytes_accessed=2**20, transcendentals=0),
        )(*arrays)

    return run


def load_kernel(hidden, weight, sent, weight_out, sems):
    start = pl.multiple_of((1 - lax.axis_index("fsdp")) * weight.shape[0], 128)
    copies = [
        pltpu.make_async_copy(hidden.at[:, pl.ds(start, sent.shape[1])], sent, sems.at[0]),
        pltpu.make_async_copy(weight, weight_out, sems.at[1]),
    ]
    for copy in copies:
        copy.start()
    for copy in copies:
        copy.wait()


def late_load_kernel(rows, base, hidden, sent, sem):
    start = pl.multiple_of((1 - lax.axis_index("fsdp")) * rows + base, 128)
    copy = pltpu.make_async_copy(hidden.at[:, pl.ds(start, sent.shape[1])], sent, sem)
    copy.start()
    copy.wait()


def sent_kernel(weight, cot, *outs):
    offset = (1 - lax.axis_index("tensor") % 2) * sum(out.shape[1] for out in outs)
    for out in outs:
        rows = weight[pl.ds(pl.multiple_of(offset, 128), out.shape[1]), :]
        out[...] = matmul_t(cot[...], rows).astype(out.dtype)
        offset = offset + out.shape[1]


def kept_kernel(weight, own, other, *outs):
    tokens = own.shape[0]
    offset = (lax.axis_index("tensor") % 2) * sum(out.shape[1] for out in outs)
    for out in outs:
        rows = weight[pl.ds(pl.multiple_of(offset, 128), out.shape[1]), :]
        out[:tokens] = matmul_t(own[...], rows)
        out[tokens:] = matmul_t(other[...], rows)
        offset = offset + out.shape[1]


def others_kernel(kept, got, out):
    out[...] = (kept[out.shape[0] :] + got[...].astype(jnp.float32)).astype(out.dtype)


def at_home(shape):
    home = (lax.axis_index("fsdp") == lax.axis_index("tensor") // 2).astype(jnp.int32)
    return jnp.full(shape, home, jnp.int32) == 1


def select_kernel(kept, got, crossed, away, stay):
    mine = (kept[: away.shape[0]] + got[...].astype(jnp.float32)).astype(away.dtype)
    home = at_home(away.shape)
    away[...] = jnp.where(home, crossed[...], mine)
    stay[...] = jnp.where(home, mine, crossed[...])


def final_parts(base, parts, out, made, sems):
    copies, offset = [], 0
    for i in range(len(parts) // 2):
        stay, last = parts[2 * i : 2 * i + 2]
        columns = pl.ds(offset, stay.shape[1])
        total = stay[...].astype(jnp.float32) + last[...].astype(jnp.float32)
        made[:, columns] = total.astype(made.dtype)
        where = pl.ds(base + offset, stay.shape[1])
        copies.append(pltpu.make_async_copy(made.at[:, columns], out.at[:, where], sems.at[i]))
        copies[i].start()
        offset += stay.shape[1]
    return copies


def final_kernel(base, count, *refs):
    for copy in final_parts(base, refs[: 2 * count], *refs[-3:]):
        copy.wait()


def last_kernel(base, count, *refs):
    parts, (own_part, back) = refs[: 2 * count], refs[2 * count : 2 * count + 2]
    out, keys, made, sems, keys_made, keys_sem = refs[-6:]
    keys_made[...] = (own_part[...] + back[...].astype(jnp.float32)).astype(keys.dtype)
    copies = [pltpu.make_async_copy(keys_made, keys, keys_sem)]
    copies[0].start()
    copies += final_parts(base, parts, out, made, sems)
    for copy in copies:
        copy.wait()


def weights_kernel(base, width, count, hidden, own_cot, other_cot, *rest):
    moved, (out, left, made, sems) = rest[:count], rest[-4:]
    start = pl.multiple_of(lax.axis_index("fsdp") * out.shape[0] + base, 128)
    blocks = [(piece, at) for piece in moved for at in range(0, piece.shape[1], width)]
    reads, writes = [], []
    for b in range(len(blocks)):
        columns = pl.ds(start + b * width, width)
        reads.append(pltpu.make_async_copy(hidden.at[:, columns], left.at[b], sems.at[0, b]))
        reads[b].start()
    for b, (piece, at) in enumerate(blocks):
        reads[b].wait()
        right = piece[:, at : at + width]
        total = matmul_first(left[b], own_cot[...]) + matmul_first(right, other_cot[...])
        made[b] = total.astype(made.dtype)
        writes.append(
            pltpu.make_async_copy(made.at[b], out.at[pl.ds(base + b * width, width)], sems.at[1, b])
        )
        writes[b].start()
    for copy in writes:
        copy.wait()


def weight_rows(hidden, moved, own_cot, other_cot, rows, base, before):
    tokens, head_cols = own_cot.shape
    columns = sum(piece.shape[1] for piece in moved)
    width = math.gcd(1024, *(piece.shape[1] for piece in moved))
    blocks = columns // width
    kept = () if before is None else (before,)
    run = call(
        functools.partial(weights_kernel, base, width, len(moved)),
        jax.ShapeDtypeStruct((rows, head_cols), jnp.bfloat16),
        [HBM] + [VMEM] * (2 + len(moved)) + [HBM] * len(kept),
        HBM,
        [
            pltpu.VMEM((blocks, tokens, width), hidden.dtype),
            pltpu.VMEM((blocks, width, head_cols), jnp.bfloat16),
            pltpu.SemaphoreType.DMA((2, blocks)),
        ],
        {3 + len(moved): 0} if kept else {},
        4 * tokens * head_cols * columns,
    )
    return run(hidden, own_cot, other_cot, *moved, *kept)


def keys_own_kernel(hidden, moved, weight, own_part, moved_part, left, sem):
    start = pl.multiple_of(lax.axis_index("fsdp") * weight.shape[0], 128)
    copy = pltpu.make_async_copy(hidden.at[:, pl.ds(start, left.shape[1])], left, sem)
    copy.start()
    half = moved.shape[1]
    moved_part[...] = jnp.dot(moved[...], weight[:half], preferred_element_type=jnp.float32)
    copy.wait()
    own_part[...] = jnp.dot(left[...], weight[...], preferred_element_type=jnp.float32)


def keys_sent_kernel(part, weight, *rest):
    moved, out = rest[:-1], rest[-1]
    total = part[...]
    base = weight.shape[0] - sum(piece.shape[1] for piece in moved)
    for piece in moved:
        rows = weight[base : base + piece.shape[1]]
        total = total + jnp.dot(piece[...], rows, preferred_element_type=jnp.float32)
        base += piece.shape[1]
    out[...] = total.astype(out.dtype)


def outer_first_kernel(due_index, counts, grads, params, moment, packed, sems):
    rows, own = grads.shape[0], params.shape[1]
    due, slot = due_index[0], lax.axis_index("replica")
    reads = [
        pltpu.make_async_copy(source.at[due], packed.at[pl.ds(rows + i * own, own)], sems.at[i])
        for i, source in enumerate((params, moment))
    ]
    for copy in reads:
        copy.start()
    total = jnp.float32(0)
    for i in range(counts.shape[0]):
        total = total + counts[i].astype(jnp.float32)
    shape = (1, grads.shape[1])
    share = jnp.full(shape, counts[slot].astype(jnp.float32)) / jnp.full(shape, total)
    packed[:rows] = grads[...] * share
    for copy in reads:
        copy.wait()


def lower_half(bit, shape):
    mine = (lax.axis_index("replica") // bit) % 2
    return jnp.full(shape, mine, jnp.int32) == 0


def outer_join_kernel(rows, packed, got, out):
    held = packed.shape[0] - rows
    out[:rows] = packed[:rows] + got[:rows]
    here = lower_half(1, (held, packed.shape[1]))
    out[rows : rows + held] = jnp.where(here, packed[rows:], got[rows:])
    out[rows + held :] = jnp.where(here, got[rows:], packed[rows:])


def outer_last_kernel(rows, own, packed, got, params_out, moment_out):
    average = packed[:rows] + got[:rows]
    owners = rows // own
    here = lower_half(2, (2 * own, packed.shape[1]))
    for i in range(owners):
        low = i < owners // 2
        base = rows + (i % (owners // 2)) * 2 * own
        ours, theirs = packed[base : base + 2 * own], got[base : base + 2 * own]
        held = jnp.where(here, ours, theirs) if low else jnp.where(here, theirs, ours)
        part = average[i * own : (i + 1) * own]
        updated, moment_new = stepped(part, held[:own], held[own:])
        params_out[i * own : (i + 1) * own] = updated

        @pl.when(lax.axis_index("replica") == i)
        def _():
            moment_out[...] = moment_new


def outer_step(pseudo_grads, outer_params, outer_moment, token_counts, due_index):
    grads = pseudo_grads[0]
    rows, columns = grads.shape
    own = outer_params.shape[1]

    def packed_shape(owners):
        return jax.ShapeDtypeStruct((rows + 2 * own * owners, columns), jnp.float32)

    specs = [SMEM, SMEM, VMEM, HBM, HBM]
    sems = [pltpu.SemaphoreType.DMA((2,))]
    packed = call(outer_first_kernel, packed_shape(1), specs, VMEM, sems)(
        due_index, token_counts, grads, outer_params, outer_moment
    )
    got = flip(packed, "replica", 1)
    kernel = functools.partial(outer_join_kernel, rows)
    packed = call(kernel, packed_shape(2), [VMEM, VMEM], VMEM)(packed, got)
    got = flip(packed, "replica", 2)
    outs = (
        jax.ShapeDtypeStruct((rows, columns), jnp.bfloat16),
        jax.ShapeDtypeStruct((own, columns), jnp.float32),
    )
    kernel = functools.partial(outer_last_kernel, rows, own)
    return call(kernel, outs, [VMEM, VMEM], (VMEM, VMEM))(packed, got)


def on_device(
    hidden, key_weight, key_grad, pseudo_grads, outer_params, outer_moment, token_counts, due_index
):
    shard_rows, head_cols = key_weight.shape[1:]
    tok_rows = key_grad.shape[0]
    widths = [shard_rows * piece // sum(PIECES) for piece in PIECES]
    bases = [sum(widths[:i]) for i in range(len(widths))]
    other_cot = flip(key_grad, "fsdp", 1)
    narrow = jax.ShapeDtypeStruct((tok_rows, widths[0]), hidden.dtype)
    outs = (narrow, jax.ShapeDtypeStruct((shard_rows, head_cols), key_weight.dtype))
    sems = [pltpu.SemaphoreType.DMA((2,))]
    sent, weight = call(load_kernel, outs, [HBM] * 2, (VMEM,) * 2, sems, limit=LOAD_LIMIT)(
        hidden, key_weight[0]
    )
    moved = [flip(sent, "fsdp", 1)]
    for i in range(1, len(widths)):
        narrow = jax.ShapeDtypeStruct((tok_rows, widths[i]), hidden.dtype)
        kernel = functools.partial(late_load_kernel, shard_rows, bases[i])
        sent = call(kernel, narrow, [HBM], VMEM, [pltpu.SemaphoreType.DMA])(hidden)
        moved.append(flip(sent, "fsdp", 1))

    block = shard_rows // 2
    chunks = [block * part // sum(PARTS) for part in PARTS]
    count, flops = len(chunks), 4 * tok_rows * head_cols * block
    part = [jax.ShapeDtypeStruct((tok_rows, chunk), jnp.bfloat16) for chunk in chunks]
    both = [jax.ShapeDtypeStruct((2 * tok_rows, chunk), jnp.float32) for chunk in chunks]
    got_own, got = [
        [
            flip(gone, "tensor", 1)
            for gone in call(sent_kernel, part, [VMEM] * 2, [VMEM] * count, flops=flops)(weight, cot)
        ]
        for cot in (key_grad, other_cot)
    ]
    kept = call(kept_kernel, both, [VMEM] * 3, [VMEM] * count, flops=flops)(
        weight, key_grad, other_cot
    )
    ends = []
    for c in range(count):
        others = call(others_kernel, part[c], [VMEM] * 2, VMEM)(kept[c], got[c])
        crossed = flip(others, "fsdp", 1)
        run = call(select_kernel, (part[c],) * 2, [VMEM] * 3, (VMEM,) * 2)
        away, stay = run(kept[c], got_own[c], crossed)
        ends.append((stay, flip(away, "tensor", 2)))
    sums = jax.ShapeDtypeStruct((tok_rows, head_cols), jnp.float32)
    own_part, moved_part = call(
        keys_own_kernel,
        (sums, sums),
        [HBM, VMEM, VMEM],
        (VMEM, VMEM),
        [pltpu.VMEM((tok_rows, shard_rows), hidden.dtype), pltpu.SemaphoreType.DMA],
    )(hidden, moved[0], weight)
    part = jax.ShapeDtypeStruct((tok_rows, head_cols), jnp.bfloat16)
    sums_sent = call(keys_sent_kernel, part, [VMEM] * (1 + len(moved)), VMEM)(
        moved_part, weight, *moved[1:]
    )
    back = flip(sums_sent, "fsdp", 1)

    weight_grad = None
    for group in GRADS:
        pieces = [moved[p] for p in group]
        weight_grad = weight_rows(
            hidden, pieces, key_grad, other_cot, shard_rows, bases[group[0]], weight_grad
        )

    fresh_params, fresh_moment = outer_step(
        pseudo_grads, outer_params, outer_moment, token_counts, due_index
    )

    hidden_grad, base = None, 0
    for i, group in enumerate(FINALS):
        ending = i == len(FINALS) - 1
        before = () if hidden_grad is None else (hidden_grad,)
        parts = [array for c in group for array in ends[c]]
        width = sum(chunks[c] for c in group)
        extra = (own_part, back) if ending else ()
        outs = (jax.ShapeDtypeStruct((tok_rows, block), jnp.bfloat16),)
        kernel, room = functools.partial(final_kernel, base, len(group)), []
        if ending:
            outs += (part,)
            room = [pltpu.VMEM(part.shape, part.dtype), pltpu.SemaphoreType.DMA]
            kernel = functools.partial(last_kernel, base, len(group))
        run = call(
            kernel,
            outs,
            [VMEM] * (len(parts) + len(extra)) + [HBM] * len(before),
            (HBM,) * len(outs),
            [pltpu.VMEM((tok_rows, width), jnp.bfloat16), pltpu.SemaphoreType.DMA((len(group),))] + room,
            {len(parts) + len(extra): 0} if before else {},
        )
        hidden_grad, *others = run(*parts, *extra, *before)
        base += width
    keys = others[0]
    return (keys, weight_grad[None], hidden_grad, fresh_params, fresh_moment)


def on_device_any(
    hidden, key_weight, key_grad, pseudo_grads, outer_params, outer_moment, token_counts, due_index
):
    weight = key_weight[0]
    block_rows = lax.all_gather(weight, "fsdp", axis=0, tiled=True)
    keys = jnp.dot(hidden, block_rows, preferred_element_type=jnp.float32).astype(jnp.bfloat16)
    input_part = matmul_t(key_grad, block_rows).astype(jnp.bfloat16)
    moved = lax.all_to_all(hidden, "fsdp", split_axis=1, concat_axis=0, tiled=True)
    cot_all = lax.all_gather(key_grad, "fsdp", axis=0, tiled=True)
    weight_grad = matmul_first(moved, cot_all).astype(jnp.bfloat16)[None]
    hidden_grad = lax.psum_scatter(input_part, "tensor", scatter_dimension=1, tiled=True)
    average = lax.psum_scatter(
        pseudo_grads[0] * share_of(token_counts), "replica", scatter_dimension=0, tiled=True
    )
    updated, moment_new = stepped(average, *due_rows(outer_params, outer_moment, due_index))
    gathered = lax.all_gather(updated, "replica", axis=0, tiled=True)
    return (keys, weight_grad, hidden_grad, gathered, moment_new)


def solution(mesh):
    sizes = mesh.shape
    fits = sizes["fsdp"] == 2 and sizes["tensor"] == 4 and sizes["replica"] == 4

    def step(*arrays):
        return (on_device if fits else on_device_any)(*arrays)

    return jax.shard_map(
        step,
        mesh=mesh,
        in_specs=(
            P(("replica", "fsdp"), None),
            P("replica", "fsdp", "tensor"),
            P(("replica", "fsdp"), "tensor"),
            P("replica", "fsdp", "tensor"),
            P(None, ("fsdp", "replica"), "tensor"),
            P(None, ("fsdp", "replica"), "tensor"),
            P(),
            P(),
        ),
        out_specs=(
            P(("replica", "fsdp"), "tensor"),
            P("replica", "fsdp", "tensor"),
            P(("replica", "fsdp"), "tensor"),
            P("fsdp", "tensor"),
            P(("fsdp", "replica"), "tensor"),
        ),
        check_vma=False,
    )
```
